128 devices in a mesh: shard: 16 (over y, z), tp: 8 (over x, core).
Axes of the slice: x: 4, y: 4, z: 4, core: 2. Of those that a mesh axis runs over, the one named last changes fastest.
Arguments:
- gradient: bfloat16 [4096, 16384], P('shard', 'tp'), may hold values from -2 to 2
- table: int32 [256, 3], replicated, may hold values from 0 to 127, as said below
- left_stat: bfloat16 [384, 512, 512], P(('shard', 'tp')), as said below
- right_stat: bfloat16 [384, 512, 512], P(('shard', 'tp')), as said below
- left_basis: bfloat16 [384, 512, 512], P(('shard', 'tp')), may hold values from -0.25 to 0.25
- right_basis: bfloat16 [384, 512, 512], P(('shard', 'tp')), may hold values from -0.25 to 0.25
- moment: bfloat16 [384, 512, 512], P(('shard', 'tp')), may hold values from -2 to 2
- second: float32 [384, 512, 512], P(('shard', 'tp')), may hold values from 0.02 to 0.2
Outputs:
- update: bfloat16 [4096, 16384], P('shard', 'tp')
- new_left: bfloat16 [384, 512, 512], P(('shard', 'tp'))
- new_right: bfloat16 [384, 512, 512], P(('shard', 'tp'))
- new_moment: bfloat16 [384, 512, 512], P(('shard', 'tp'))
- new_second: float32 [384, 512, 512], P(('shard', 'tp'))
The draws below stay inside these ranges and needn't reach their ends.
Inputs may be any that keep to these rules, and one draw needn't show every extreme that they name: `table`: column 0 is a block row below 8, column 1 a block column below 32, column 2 an owner device below 128; every block appears in exactly one row; each device owns between 1 and 3 blocks, and some device owns exactly 3. `left_stat`: Symmetric. `right_stat`: Symmetric.
All inputs are finite; a program needn't handle non-finite values.
Results may differ from the reference program's by a relative error of at most 0.0085.
Values may be sent and summed in bfloat16 or wider, within the bound.
No kernel may reach another device: no remote copies, remote signals or barrier semaphores. Data moves between devices by JAX's collectives and lax.ppermute only.
A program may use at most 128 MiB of HBM per device.

```python
import math
import jax
import jax.numpy as jnp
from jax import lax

ROWS = 4096
COLS = 16384
BLOCK = 512
NDEV = 128
NBR = 8
NBC = 32
NBLK = 256
OWN_MEAN = 2
SLOTS = 3


def stat_draw(key, salt):
    key = jax.random.fold_in(key, salt)
    first_key, second_key = jax.random.split(key)
    count = NDEV * SLOTS
    diagonal = jax.random.uniform(first_key, (count, BLOCK), jnp.float32, 1.0, 2.0)
    noise = jax.random.normal(second_key, (count, BLOCK, BLOCK), jnp.float32)
    symmetric = (noise + jnp.swapaxes(noise, 1, 2)) * (0.25 / jnp.sqrt(jnp.float32(BLOCK)))
    return symmetric + jnp.eye(BLOCK, dtype=jnp.float32)[None, :, :] * diagonal[:, None, :]


def draw_left_stat(key, part):
    return stat_draw(key, 11).astype(jnp.bfloat16)


def draw_right_stat(key, part):
    return stat_draw(key, 23).astype(jnp.bfloat16)


def draw_table(key, part):
    keys = jax.random.split(key, 4)
    reach = (OWN_MEAN + 1) // 2
    halfway = NDEV // 2
    shifts = jax.random.randint(keys[0], (halfway,), 0, reach + 1)
    shifts = shifts.at[0].set(reach)
    counts = jnp.concatenate([OWN_MEAN + shifts, OWN_MEAN - shifts])
    counts = counts[jax.random.permutation(keys[1], NDEV)]
    bounds = jnp.cumsum(counts)
    places = jnp.arange(NBLK, dtype=jnp.int32)
    owner_of = jnp.sum((bounds[None, :] <= places[:, None]).astype(jnp.int32), axis=1)
    blocks = jax.random.permutation(keys[2], NBLK).astype(jnp.int32)
    order = jax.random.permutation(keys[3], NBLK)
    owners = owner_of[order]
    return jnp.stack([blocks // NBC, blocks % NBC, owners], axis=1).astype(jnp.int32)


def level_of(key, extent, shards, low, top_value):
    level = 1.0
    for position, parts in shards:
        heights = jax.random.uniform(jax.random.fold_in(jax.random.fold_in(key, 6), position), (parts,), jnp.float32, low / len(shards), top_value / len(shards))
        level = level * jnp.repeat(jnp.exp(heights), extent[position] // parts).reshape((-1,) + (1,) * (len(extent) - 1 - position))
    return level


def gaussian(own_key, extent, width, bound, cuts=(), kind=jnp.bfloat16):
    level = level_of(own_key, extent, cuts, -0.22, 0.18) if cuts else 1.0
    array = jax.random.normal(own_key, extent, jnp.float32) * width * level
    return jnp.minimum(jnp.maximum(array, -bound), bound).astype(kind)


def setup_inputs(seed: int = 0) -> dict:
    arg_keys = jax.random.split(jax.random.key(seed), 9)
    return {
        "gradient": gaussian(arg_keys[0], (ROWS, COLS), 0.25, 2.0, ((0, 16), (1, 8))),
        "table": draw_table(jax.random.fold_in(arg_keys[8], 71), 0),
        "left_stat": draw_left_stat(jax.random.fold_in(arg_keys[8], 71), 0),
        "right_stat": draw_right_stat(jax.random.fold_in(arg_keys[8], 71), 0),
        "left_basis": gaussian(arg_keys[4], (NDEV * SLOTS, BLOCK, BLOCK), BLOCK ** -0.5, 0.25, ((0, 128),)),
        "right_basis": gaussian(arg_keys[5], (NDEV * SLOTS, BLOCK, BLOCK), BLOCK ** -0.5, 0.25, ((0, 128),)),
        "moment": gaussian(arg_keys[6], (NDEV * SLOTS, BLOCK, BLOCK), 0.25, 2.0, ((0, 128),)),
        "second": jnp.clip(jnp.exp(math.log(0.2) - 2.3025851 * jax.random.uniform(arg_keys[7], (NDEV * SLOTS, BLOCK, BLOCK), jnp.float32) ** level_of(arg_keys[7], (NDEV * SLOTS, BLOCK, BLOCK), ((0, 128),), -0.2, 0.2)), 0.02, 0.2),
    }


beta_moment = 0.9
beta_second = 0.95
beta_stats = 0.95
epsilon = 1e-08

def slot_table(table, slots):
    owners = table[:, 2]
    count = owners.shape[0]
    order = jnp.arange(count, dtype=jnp.int32)
    earlier = (owners[None, :] == owners[:, None]) & (order[None, :] < order[:, None])
    slot_rank = lax.optimization_barrier(jnp.sum(earlier.astype(jnp.int32), axis=1)).astype(jnp.int32)
    return (owners * slots + slot_rank).astype(jnp.int32)

def precondition(grad_block, left, right, left_q, right_q, first, squares):
    left_new = (beta_stats * left.astype(jnp.float32) + (1.0 - beta_stats) * jnp.dot(grad_block, grad_block.T, preferred_element_type=jnp.float32)).astype(jnp.bfloat16)
    right_new = (beta_stats * right.astype(jnp.float32) + (1.0 - beta_stats) * jnp.dot(grad_block.T, grad_block, preferred_element_type=jnp.float32)).astype(jnp.bfloat16)
    first_new = (beta_moment * first.astype(jnp.float32) + (1.0 - beta_moment) * grad_block.astype(jnp.float32)).astype(jnp.bfloat16)
    left_grad = jnp.dot(left_q.T, grad_block, preferred_element_type=jnp.float32).astype(jnp.bfloat16)
    rotated = jnp.dot(left_grad, right_q, preferred_element_type=jnp.float32)
    squares_new = beta_second * squares + (1.0 - beta_second) * rotated * rotated
    left_first = jnp.dot(left_q.T, first_new, preferred_element_type=jnp.float32).astype(jnp.bfloat16)
    first_rot = jnp.dot(left_first, right_q, preferred_element_type=jnp.float32)
    scaled = (first_rot / (jnp.sqrt(squares_new) + epsilon)).astype(jnp.bfloat16)
    back = jnp.dot(left_q, scaled, preferred_element_type=jnp.float32).astype(jnp.bfloat16)
    result = jnp.dot(back, right_q.T, preferred_element_type=jnp.float32).astype(jnp.bfloat16)
    return (result, left_new, right_new, first_new, squares_new)

def reference(gradient, table, left_stat, right_stat, left_basis, right_basis, moment, second):
    tiles = gradient.reshape(NBR, BLOCK, NBC, BLOCK).transpose(0, 2, 1, 3).reshape(NBLK, BLOCK, BLOCK)
    state_row = slot_table(table, SLOTS)
    block_id = (table[:, 0] * NBC + table[:, 1]).astype(jnp.int32)

    def one_block(index):
        slot = state_row[index]
        return precondition(tiles[block_id[index]], left_stat[slot], right_stat[slot], left_basis[slot], right_basis[slot], moment[slot], second[slot])
    results = lax.map(one_block, jnp.arange(NBLK, dtype=jnp.int32))
    block_updates, left_rows, right_rows, first_rows, square_rows = results
    new_left = left_stat.at[state_row].set(left_rows)
    new_right = right_stat.at[state_row].set(right_rows)
    new_moment = moment.at[state_row].set(first_rows)
    new_second = second.at[state_row].set(square_rows)
    placed = jnp.zeros((NBLK, BLOCK, BLOCK), jnp.bfloat16).at[block_id].set(block_updates)
    update = placed.reshape(NBR, NBC, BLOCK, BLOCK).transpose(0, 2, 1, 3).reshape(ROWS, COLS)
    return (update, new_left, new_right, new_moment, new_second)
```

```python
import functools

import jax
import jax.numpy as jnp
from jax import lax
from jax.experimental import pallas as pl
from jax.experimental.pallas import tpu as pltpu
from jax.sharding import PartitionSpec as P

beta_moment = 0.9
beta_second = 0.95
beta_stats = 0.95
epsilon = 1e-08

AXES = ("shard", "tp")
SUB, LANE = 8, 128
VMEM = pl.BlockSpec(memory_space=pltpu.VMEM)
SMEM = pl.BlockSpec(memory_space=pltpu.SMEM)


def exchange(array):
    return lax.all_to_all(array, AXES, split_axis=0, concat_axis=0, tiled=True)


def state_rows(table, slots):
    owners = table[:, 2]
    order = jnp.arange(owners.shape[0], dtype=jnp.int32)
    earlier = (owners[None, :] == owners[:, None]) & (order[None, :] < order[:, None])
    return owners * slots + jnp.sum(earlier.astype(jnp.int32), axis=1)


def pack_kernel(grad_ref, out_ref):
    tile_cols, tile_rows, blocks = out_ref.shape[:3]
    for j in range(blocks):
        for c in range(tile_cols):
            at = (j * tile_cols + c) * LANE
            out_ref[c, :, j] = grad_ref[:, at : at + LANE].reshape(tile_rows, SUB, LANE)


def unpack_kernel(in_ref, out_ref):
    tile_cols, tile_rows, blocks = in_ref.shape[:3]
    for j in range(blocks):
        for c in range(tile_cols):
            at = (j * tile_cols + c) * LANE
            out_ref[:, at : at + LANE] = in_ref[c, :, j].reshape(tile_rows * SUB, LANE)


def to_owner_kernel(half_step, grid_ref, slot_ref, in_ref, out_ref):
    halves = out_ref.shape[0] // 2
    out_ref[...] = jnp.zeros_like(out_ref)

    def body(n, carry):
        a = grid_ref[n]
        b = slot_ref[n] * 2
        out_ref[b] = in_ref[a]
        out_ref[b + 1] = in_ref[a + half_step]
        return carry

    lax.fori_loop(0, grid_ref.shape[0], body, 0, unroll=8)


def to_grid_kernel(half_step, grid_ref, slot_ref, in_ref, out_ref):
    def body(n, carry):
        a = grid_ref[n]
        b = slot_ref[n] * 2
        out_ref[a] = in_ref[b]
        out_ref[a + half_step] = in_ref[b + 1]
        return carry

    lax.fori_loop(0, grid_ref.shape[0], body, 0, unroll=8)


def prep_kernel(left_q_ref, right_q_ref, first_ref, left_t_ref, first_rot_ref):
    left_t = left_q_ref[0].T
    left_t_ref[0] = left_t
    part = jnp.dot(left_t, first_ref[0], preferred_element_type=jnp.float32).astype(jnp.bfloat16)
    first_rot_ref[0] = jnp.dot(part, right_q_ref[0], preferred_element_type=jnp.float32)


def slot_kernel(
    count_ref, grad_ref, left_t_ref, left_q_ref, right_q_ref, first_rot_ref, second_ref,
    block_ref, second_out_ref, result_ref,
):
    tile_cols, tile_rows, _, halves = grad_ref.shape[:4]
    high = tile_rows * SUB
    for c in range(tile_cols):
        for h in range(halves):
            block_ref[0, h * high : (h + 1) * high, c * LANE : (c + 1) * LANE] = grad_ref[
                c, :, 0, h
            ].reshape(high, LANE)
    grad = block_ref[0]
    left_grad = jnp.dot(left_t_ref[0], grad, preferred_element_type=jnp.float32).astype(jnp.bfloat16)
    rotated = jnp.dot(left_grad, right_q_ref[0], preferred_element_type=jnp.float32)
    first_rot = beta_moment * first_rot_ref[0] + (1.0 - beta_moment) * rotated
    squares = second_ref[0]
    squares_new = beta_second * squares + (1.0 - beta_second) * rotated * rotated
    kept = pl.program_id(0) < count_ref[0]
    second_out_ref[0] = jnp.where(kept, squares_new, squares)
    scaled = (first_rot / (jnp.sqrt(squares_new) + epsilon)).astype(jnp.bfloat16)
    back = jnp.dot(left_q_ref[0], scaled, preferred_element_type=jnp.float32).astype(jnp.bfloat16)
    result = lax.dot_general(
        back, right_q_ref[0], (((1,), (1,)), ((), ())), preferred_element_type=jnp.float32
    ).astype(jnp.bfloat16)
    for c in range(tile_cols):
        for h in range(halves):
            result_ref[c, :, 0, h] = result[
                h * high : (h + 1) * high, c * LANE : (c + 1) * LANE
            ].reshape(tile_rows, SUB, LANE)


def per_slot(side):
    return pl.BlockSpec((1, side, side), lambda k: (k, 0, 0))


def shards(gradient, table, left_stat, right_stat, left_basis, right_basis, moment, second):
    dev_count = lax.axis_size(AXES)
    rows, cols = gradient.shape
    slots, side, _ = left_stat.shape
    halves = side // rows
    tile_cols = side // LANE
    tile_rows = rows // SUB
    blocks = cols // side
    block_cols = lax.axis_size("tp") * blocks
    bf16, f32 = jnp.bfloat16, jnp.float32

    packed = pl.pallas_call(
        pack_kernel,
        out_shape=jax.ShapeDtypeStruct((tile_cols, tile_rows, blocks, SUB, LANE), bf16),
        in_specs=[VMEM],
        out_specs=VMEM,
    )(gradient)
    spread = exchange(packed.reshape(dev_count, blocks, SUB, LANE))

    slot_row = state_rows(table, slots)
    grid_row = table[:, 0] * (halves * block_cols) + table[:, 1]
    myself = lax.axis_index(AXES)
    count = jnp.sum((table[:, 2] == myself).astype(jnp.int32)).reshape(1)

    left_t, first_rot = pl.pallas_call(
        prep_kernel,
        grid=(slots,),
        out_shape=[
            jax.ShapeDtypeStruct((slots, side, side), bf16),
            jax.ShapeDtypeStruct((slots, side, side), f32),
        ],
        in_specs=[per_slot(side)] * 3,
        out_specs=[per_slot(side)] * 2,
        cost_estimate=pl.CostEstimate(
            flops=4 * slots * side**3, bytes_accessed=12 * slots * side**2, transcendentals=0
        ),
    )(left_basis, right_basis, moment)

    outbox = pl.pallas_call(
        functools.partial(to_owner_kernel, block_cols),
        out_shape=jax.ShapeDtypeStruct((dev_count * slots * halves, SUB, LANE), bf16),
        in_specs=[SMEM, SMEM, VMEM],
        out_specs=VMEM,
    )(grid_row, slot_row, spread.reshape(dev_count * blocks, SUB, LANE))
    inbox = exchange(outbox.reshape(dev_count, slots, halves, SUB, LANE))

    pieces = pl.BlockSpec(
        (tile_cols, tile_rows, 1, halves, SUB, LANE), lambda k: (0, 0, k, 0, 0, 0)
    )
    grad_blocks, new_second, results = pl.pallas_call(
        slot_kernel,
        grid=(slots,),
        out_shape=[
            jax.ShapeDtypeStruct((slots, side, side), bf16),
            jax.ShapeDtypeStruct((slots, side, side), f32),
            jax.ShapeDtypeStruct((tile_cols, tile_rows, slots, halves, SUB, LANE), bf16),
        ],
        in_specs=[SMEM, pieces] + [per_slot(side)] * 5,
        out_specs=[per_slot(side)] * 2 + [pieces],
        cost_estimate=pl.CostEstimate(
            flops=8 * slots * side**3, bytes_accessed=20 * slots * side**2, transcendentals=0
        ),
    )(
        count,
        inbox.reshape(tile_cols, tile_rows, slots, halves, SUB, LANE),
        left_t,
        left_basis,
        right_basis,
        first_rot,
        second,
    )
    returned = exchange(results.reshape(dev_count, slots, halves, SUB, LANE))

    kept = (jnp.arange(slots, dtype=jnp.int32) < count)[:, None, None]
    new_left = jnp.where(
        kept,
        (
            beta_stats * left_stat.astype(f32)
            + (1.0 - beta_stats)
            * jnp.einsum("sik,sjk->sij", grad_blocks, grad_blocks, preferred_element_type=f32)
        ).astype(bf16),
        left_stat,
    )
    new_right = jnp.where(
        kept,
        (
            beta_stats * right_stat.astype(f32)
            + (1.0 - beta_stats)
            * jnp.einsum("ski,skj->sij", grad_blocks, grad_blocks, preferred_element_type=f32)
        ).astype(bf16),
        right_stat,
    )
    new_moment = jnp.where(
        kept,
        (
            beta_moment * moment.astype(f32) + (1.0 - beta_moment) * grad_blocks.astype(f32)
        ).astype(bf16),
        moment,
    )

    gathered = pl.pallas_call(
        functools.partial(to_grid_kernel, block_cols),
        out_shape=jax.ShapeDtypeStruct((dev_count * blocks, SUB, LANE), bf16),
        in_specs=[SMEM, SMEM, VMEM],
        out_specs=VMEM,
    )(grid_row, slot_row, returned.reshape(dev_count * slots * halves, SUB, LANE))
    arrived = exchange(gathered.reshape(dev_count, blocks, SUB, LANE))
    update = pl.pallas_call(
        unpack_kernel,
        out_shape=jax.ShapeDtypeStruct((rows, cols), bf16),
        in_specs=[VMEM],
        out_specs=VMEM,
    )(arrived.reshape(tile_cols, tile_rows, blocks, SUB, LANE))
    return (update, new_left, new_right, new_moment, new_second)


def solution(mesh):
    states = P(AXES, None, None)
    window = P("shard", "tp")
    return jax.shard_map(
        shards,
        mesh=mesh,
        in_specs=(window, P()) + (states,) * 6,
        out_specs=(window,) + (states,) * 4,
        check_vma=False,
    )
```

```python
import functools

import jax
import jax.numpy as jnp
from jax import lax
from jax.experimental import pallas as pl
from jax.experimental.pallas import tpu as pltpu
from jax.sharding import PartitionSpec as P

beta_moment = 0.9
beta_second = 0.95
beta_stats = 0.95
epsilon = 1e-08

AXES = ("shard", "tp")
SUB, LANE = 8, 128
VMEM = pl.BlockSpec(memory_space=pltpu.VMEM)
CHUNKS = 8
SMALL = pltpu.CompilerParams(vmem_limit_bytes=8 << 20)
HBM = pl.BlockSpec(memory_space=pltpu.HBM)
SMEM = pl.BlockSpec(memory_space=pltpu.SMEM)


def exchange(array):
    return lax.all_to_all(array, AXES, split_axis=0, concat_axis=0, tiled=True)


def state_rows(table, slots):
    owners = table[:, 2]
    order = jnp.arange(owners.shape[0], dtype=jnp.int32)
    earlier = (owners[None, :] == owners[:, None]) & (order[None, :] < order[:, None])
    return owners * slots + jnp.sum(earlier.astype(jnp.int32), axis=1)


def pack_kernel(grad_ref, out_ref, held_ref, load_sems, store_sems):
    tile_cols, _, blocks = out_ref.shape[:3]
    loads, stores = [], []
    for j in range(blocks):
        for c in range(tile_cols):
            at = j * tile_cols + c
            lanes = slice(at * LANE, (at + 1) * LANE)
            loads.append(
                pltpu.make_async_copy(grad_ref.at[:, :, lanes], held_ref.at[at], load_sems.at[at])
            )
            stores.append(
                pltpu.make_async_copy(held_ref.at[at], out_ref.at[c, :, j], store_sems.at[at])
            )
            loads[-1].start()
    for load, store in zip(loads, stores):
        load.wait()
        store.start()
    for store in stores:
        store.wait()


def unpack_kernel(in_ref, out_ref, sems):
    tile_cols, _, blocks = in_ref.shape[:3]
    copies = []
    for j in range(blocks):
        for c in range(tile_cols):
            at = j * tile_cols + c
            copies.append(
                pltpu.make_async_copy(
                    in_ref.at[c, :, j], out_ref.at[:, :, at * LANE : (at + 1) * LANE], sems.at[at]
                )
            )
            copies[-1].start()
    for copy in copies:
        copy.wait()


def to_owner_kernel(half_step, cell_ref, in_ref, out_hbm, out_ref, sems):
    chunks = sems.shape[0]
    rows = cell_ref.shape[0] // chunks
    stores = []
    for r in range(chunks):
        for n in range(r * rows, (r + 1) * rows):
            a = cell_ref[n]
            out_ref[2 * n] = in_ref[a]
            out_ref[2 * n + 1] = in_ref[a + half_step]
        at = pl.ds(2 * r * rows, 2 * rows)
        stores.append(pltpu.make_async_copy(out_ref.at[at], out_hbm.at[at], sems.at[r]))
        stores[-1].start()
    for store in stores:
        store.wait()


def to_grid_kernel(half_step, row_ref, in_ref, out_hbm, out_ref, sems):
    stores = []
    for r in range(row_ref.shape[0] // half_step):
        base = r * 2 * half_step
        for c in range(half_step):
            b = row_ref[r * half_step + c] * 2
            out_ref[base + c] = in_ref[b]
            out_ref[base + c + half_step] = in_ref[b + 1]
        at = pl.ds(base, 2 * half_step)
        stores.append(pltpu.make_async_copy(out_ref.at[at], out_hbm.at[at], sems.at[r]))
        stores[-1].start()
    for store in stores:
        store.wait()


def prep_kernel(left_q_ref, right_q_ref, first_ref, left_t_ref, first_rot_ref):
    left_t = left_q_ref[0].T
    left_t_ref[0] = left_t
    part = jnp.dot(left_t, first_ref[0], preferred_element_type=jnp.float32).astype(jnp.bfloat16)
    first_rot_ref[0] = beta_moment * jnp.dot(
        part, right_q_ref[0], preferred_element_type=jnp.float32
    )


def slot_kernel(
    count_ref, grad_ref, left_t_hbm, right_q_hbm, first_rot_hbm, second_hbm, left_q_hbm,
    block_hbm, second_out_hbm, result_hbm,
    left_t_ref, right_q_ref, first_rot_ref, second_ref, left_q_ref,
    block_ref, second_out_ref, rotated_ref, result_ref,
    in_sems, block_sems, second_sems, result_sems,
):
    tile_cols, tile_rows, slots, halves = grad_ref.shape[:4]
    high = tile_rows * SUB
    inputs = (
        (left_t_hbm, left_t_ref),
        (right_q_hbm, right_q_ref),
        (first_rot_hbm, first_rot_ref),
        (second_hbm, second_ref),
        (left_q_hbm, left_q_ref),
    )
    loads = [
        [
            pltpu.make_async_copy(src.at[k], dst.at[k], in_sems.at[k, i])
            for i, (src, dst) in enumerate(inputs)
        ]
        for k in range(slots)
    ]
    for row in loads:
        for load in row:
            load.start()
    stores = []

    def store(src, dst, sem):
        stores.append(pltpu.make_async_copy(src, dst, sem))
        stores[-1].start()

    def assemble(k):
        for c in range(tile_cols):
            for h in range(halves):
                block_ref[k, h * high : (h + 1) * high, c * LANE : (c + 1) * LANE] = grad_ref[
                    c, :, k, h
                ].reshape(high, LANE)
        store(block_ref.at[k], block_hbm.at[k], block_sems.at[k])

    def rotate(k):
        left_grad = jnp.dot(left_t_ref[k], block_ref[k], preferred_element_type=jnp.float32)
        rotated_ref[k % 2] = jnp.dot(
            left_grad.astype(jnp.bfloat16), right_q_ref[k], preferred_element_type=jnp.float32
        )

    def scale(k):
        rotated = rotated_ref[k % 2]
        first_rot = first_rot_ref[k] + (1.0 - beta_moment) * rotated
        old = second_ref[k]
        squares = beta_second * old + (1.0 - beta_second) * rotated * rotated
        second_out_ref[k] = squares if k == 0 else jnp.where(k < count_ref[0], squares, old)
        root = squares * lax.rsqrt(squares)
        return (first_rot / (root + epsilon)).astype(jnp.bfloat16)

    def finish(k, scaled):
        turned = lax.dot_general(
            scaled, right_q_ref[k], (((1,), (1,)), ((), ())), preferred_element_type=jnp.float32
        ).astype(jnp.bfloat16)
        result = jnp.dot(left_q_ref[k], turned, preferred_element_type=jnp.float32).astype(
            jnp.bfloat16
        )
        for h in range(halves):
            for c in range(tile_cols):
                result_ref[c, :, k, h] = result[
                    h * high : (h + 1) * high, c * LANE : (c + 1) * LANE
                ].reshape(tile_rows, SUB, LANE)
            store(result_ref.at[:, :, k, h], result_hbm.at[:, :, k, h], result_sems.at[k, h])

    def wait(k, names):
        for i in names:
            loads[k][i].wait()

    assemble(0)
    wait(0, (0, 1))
    rotate(0)
    for k in range(slots):
        wait(k, (2, 3, 4))
        if k + 1 < slots:
            assemble(k + 1)
            wait(k + 1, (0, 1))
            rotate(k + 1)
        scaled = scale(k)
        store(second_out_ref.at[k], second_out_hbm.at[k], second_sems.at[k])
        finish(k, scaled)
    for copy in stores:
        copy.wait()


def per_slot(side):
    return pl.BlockSpec((1, side, side), lambda k: (k, 0, 0))


def near(array):
    return pltpu.with_memory_space_constraint(array, pltpu.VMEM)


def far(array):
    return pltpu.with_memory_space_constraint(array, pltpu.HBM)


def shards(gradient, table, left_stat, right_stat, left_basis, right_basis, moment, second):
    dev_count = lax.axis_size(AXES)
    rows, cols = gradient.shape
    slots, side, _ = left_stat.shape
    halves = side // rows
    tile_cols = side // LANE
    tile_rows = rows // SUB
    blocks = cols // side
    block_cols = lax.axis_size("tp") * blocks
    bf16, f32 = jnp.bfloat16, jnp.float32

    packed = pl.pallas_call(
        pack_kernel,
        out_shape=pltpu.HBM((tile_cols, tile_rows, blocks, SUB, LANE), bf16),
        in_specs=[HBM],
        out_specs=HBM,
        scratch_shapes=[
            pltpu.VMEM((blocks * tile_cols, tile_rows, SUB, LANE), bf16),
            pltpu.SemaphoreType.DMA((blocks * tile_cols,)),
            pltpu.SemaphoreType.DMA((blocks * tile_cols,)),
        ],
        compiler_params=SMALL,
    )(far(gradient.reshape(tile_rows, SUB, cols)))
    spread = exchange(packed.reshape(dev_count, blocks, SUB, LANE))

    slot_row = state_rows(table, slots)
    block_id = table[:, 0] * block_cols + table[:, 1]
    cell = block_id + table[:, 0] * ((halves - 1) * block_cols)
    targets = jnp.arange(dev_count * slots, dtype=jnp.int32)
    cell_of_row = jnp.sum(
        jnp.where(slot_row[None, :] == targets[:, None], cell[None, :], 0), axis=1
    )
    places = jnp.arange(table.shape[0], dtype=jnp.int32)
    row_of_block = jnp.sum(
        jnp.where(block_id[None, :] == places[:, None], slot_row[None, :], 0), axis=1
    )
    myself = lax.axis_index(AXES)
    count = jnp.sum((table[:, 2] == myself).astype(jnp.int32)).reshape(1)

    state = (slots, side, side)
    left_t, first_rot = pl.pallas_call(
        prep_kernel,
        grid=(slots,),
        out_shape=[jax.ShapeDtypeStruct(state, bf16), jax.ShapeDtypeStruct(state, f32)],
        in_specs=[per_slot(side)] * 3,
        out_specs=[per_slot(side)] * 2,
        cost_estimate=pl.CostEstimate(
            flops=4 * slots * side**3, bytes_accessed=12 * slots * side**2, transcendentals=0
        ),
    )(left_basis, right_basis, moment)

    outbox = pl.pallas_call(
        functools.partial(to_owner_kernel, block_cols),
        out_shape=pltpu.HBM((dev_count * slots * halves, SUB, LANE), bf16),
        in_specs=[SMEM, VMEM],
        out_specs=HBM,
        scratch_shapes=[
            pltpu.VMEM((dev_count * slots * halves, SUB, LANE), bf16),
            pltpu.SemaphoreType.DMA((CHUNKS,)),
        ],
        compiler_params=SMALL,
    )(cell_of_row, near(spread.reshape(dev_count * blocks, SUB, LANE)))
    inbox = exchange(outbox.reshape(dev_count, slots, halves, SUB, LANE))

    grad_blocks, new_second, results = pl.pallas_call(
        slot_kernel,
        out_shape=[
            jax.ShapeDtypeStruct(state, bf16),
            jax.ShapeDtypeStruct(state, f32),
            pltpu.HBM((tile_cols, tile_rows, slots, halves, SUB, LANE), bf16),
        ],
        in_specs=[SMEM, VMEM] + [HBM] * 5,
        out_specs=[HBM] * 3,
        scratch_shapes=[
            pltpu.VMEM(state, bf16),
            pltpu.VMEM(state, bf16),
            pltpu.VMEM(state, f32),
            pltpu.VMEM(state, f32),
            pltpu.VMEM(state, bf16),
            pltpu.VMEM(state, bf16),
            pltpu.VMEM(state, f32),
            pltpu.VMEM((2, side, side), f32),
            pltpu.VMEM((tile_cols, tile_rows, slots, halves, SUB, LANE), bf16),
            pltpu.SemaphoreType.DMA((slots, 5)),
            pltpu.SemaphoreType.DMA((slots,)),
            pltpu.SemaphoreType.DMA((slots,)),
            pltpu.SemaphoreType.DMA((slots, halves)),
        ],
        compiler_params=pltpu.CompilerParams(vmem_limit_bytes=48 << 20),
        cost_estimate=pl.CostEstimate(
            flops=8 * slots * side**3, bytes_accessed=20 * slots * side**2, transcendentals=0
        ),
    )(
        count,
        near(inbox.reshape(tile_cols, tile_rows, slots, halves, SUB, LANE)),
        far(left_t),
        far(right_basis),
        far(first_rot),
        far(second),
        far(left_basis),
    )
    returned = exchange(results.reshape(dev_count, slots, halves, SUB, LANE))

    kept = (jnp.arange(slots, dtype=jnp.int32) < count)[:, None, None]
    new_left = jnp.where(
        kept,
        (
            beta_stats * left_stat.astype(f32)
            + (1.0 - beta_stats)
            * jnp.einsum("sik,sjk->sij", grad_blocks, grad_blocks, preferred_element_type=f32)
        ).astype(bf16),
        left_stat,
    )
    new_right = jnp.where(
        kept,
        (
            beta_stats * right_stat.astype(f32)
            + (1.0 - beta_stats)
            * jnp.einsum("ski,skj->sij", grad_blocks, grad_blocks, preferred_element_type=f32)
        ).astype(bf16),
        right_stat,
    )
    new_moment = jnp.where(
        kept,
        (
            beta_moment * moment.astype(f32) + (1.0 - beta_moment) * grad_blocks.astype(f32)
        ).astype(bf16),
        moment,
    )

    gathered = pl.pallas_call(
        functools.partial(to_grid_kernel, block_cols),
        out_shape=pltpu.HBM((dev_count * blocks, SUB, LANE), bf16),
        in_specs=[SMEM, VMEM],
        out_specs=HBM,
        scratch_shapes=[
            pltpu.VMEM((dev_count * blocks, SUB, LANE), bf16),
            pltpu.SemaphoreType.DMA((dev_count * blocks // (halves * block_cols),)),
        ],
        compiler_params=SMALL,
    )(row_of_block, near(returned.reshape(dev_count * slots * halves, SUB, LANE)))
    arrived = exchange(gathered.reshape(dev_count, blocks, SUB, LANE))
    update = pl.pallas_call(
        unpack_kernel,
        out_shape=jax.ShapeDtypeStruct((tile_rows, SUB, cols), bf16),
        in_specs=[VMEM],
        out_specs=HBM,
        scratch_shapes=[pltpu.SemaphoreType.DMA((blocks * tile_cols,))],
        compiler_params=SMALL,
    )(near(arrived.reshape(tile_cols, tile_rows, blocks, SUB, LANE))).reshape(rows, cols)
    return (update, new_left, new_right, new_moment, new_second)


def solution(mesh):
    states = P(AXES, None, None)
    window = P("shard", "tp")
    return jax.shard_map(
        shards,
        mesh=mesh,
        in_specs=(window, P()) + (states,) * 6,
        out_specs=(window,) + (states,) * 4,
        check_vma=False,
    )
```

```python
import functools

import jax
import jax.numpy as jnp
from jax import lax
from jax.experimental import pallas as pl
from jax.experimental.pallas import tpu as pltpu
from jax.sharding import PartitionSpec as P

beta_moment = 0.9
beta_second = 0.95
beta_stats = 0.95
epsilon = 1e-08

AXES = ("shard", "tp")
SUB, LANE = 8, 128
VMEM = pl.BlockSpec(memory_space=pltpu.VMEM)
PARTS = 4
CHUNKS = 8
SMALL = pltpu.CompilerParams(vmem_limit_bytes=8 << 20)
HBM = pl.BlockSpec(memory_space=pltpu.HBM)
SMEM = pl.BlockSpec(memory_space=pltpu.SMEM)


def exchange(array):
    return lax.all_to_all(array, AXES, split_axis=0, concat_axis=0, tiled=True)


def state_rows(table, slots):
    owners = table[:, 2]
    order = jnp.arange(owners.shape[0], dtype=jnp.int32)
    earlier = (owners[None, :] == owners[:, None]) & (order[None, :] < order[:, None])
    return owners * slots + jnp.sum(earlier.astype(jnp.int32), axis=1)


def pack_kernel(grad_ref, out_ref, held_ref, packed_ref, load_sems, store_sems):
    tile_cols, tile_rows, blocks = out_ref.shape[:3]
    parts = load_sems.shape[0]
    step = tile_rows // parts
    loads, stores = [], []
    for r in range(parts):
        at = pl.ds(r * step, step)
        loads.append(pltpu.make_async_copy(grad_ref.at[at], held_ref.at[at], load_sems.at[r]))
        stores.append(
            pltpu.make_async_copy(packed_ref.at[:, at], out_ref.at[:, at], store_sems.at[r])
        )
        loads[-1].start()
    for r in range(parts):
        loads[r].wait()
        rows = slice(r * step, (r + 1) * step)
        for j in range(blocks):
            for c in range(tile_cols):
                at = (j * tile_cols + c) * LANE
                packed_ref[c, rows, j] = held_ref[rows, :, at : at + LANE]
        stores[r].start()
    for store in stores:
        store.wait()


def unpack_kernel(in_ref, out_ref, sems):
    tile_cols, _, blocks = in_ref.shape[:3]
    copies = []
    for j in range(blocks):
        for c in range(tile_cols):
            at = j * tile_cols + c
            copies.append(
                pltpu.make_async_copy(
                    in_ref.at[c, :, j], out_ref.at[:, :, at * LANE : (at + 1) * LANE], sems.at[at]
                )
            )
            copies[-1].start()
    for copy in copies:
        copy.wait()


def to_owner_kernel(half_step, cell_ref, in_ref, out_hbm, out_ref, sems):
    chunks = sems.shape[0]
    rows = cell_ref.shape[0] // chunks
    stores = []
    for r in range(chunks):
        for n in range(r * rows, (r + 1) * rows):
            a = cell_ref[n]
            out_ref[2 * n] = in_ref[a]
            out_ref[2 * n + 1] = in_ref[a + half_step]
        at = pl.ds(2 * r * rows, 2 * rows)
        stores.append(pltpu.make_async_copy(out_ref.at[at], out_hbm.at[at], sems.at[r]))
        stores[-1].start()
    for store in stores:
        store.wait()


def to_grid_kernel(half_step, row_ref, in_ref, out_hbm, out_ref, sems):
    stores = []
    for r in range(row_ref.shape[0] // half_step):
        base = r * 2 * half_step
        for c in range(half_step):
            b = row_ref[r * half_step + c] * 2
            out_ref[base + c] = in_ref[b]
            out_ref[base + c + half_step] = in_ref[b + 1]
        at = pl.ds(base, 2 * half_step)
        stores.append(pltpu.make_async_copy(out_ref.at[at], out_hbm.at[at], sems.at[r]))
        stores[-1].start()
    for store in stores:
        store.wait()


def prep_kernel(
    left_q_ref, right_q_ref, first_ref, second_ref, left_t_ref, first_rot_ref, decayed_ref
):
    left_t = left_q_ref[0].T
    left_t_ref[0] = left_t
    part = jnp.dot(left_t, first_ref[0], preferred_element_type=jnp.float32).astype(jnp.bfloat16)
    first_rot_ref[0] = (2.0 * beta_moment) * jnp.dot(
        part, right_q_ref[0], preferred_element_type=jnp.float32
    )
    decayed_ref[0] = (4.0 * beta_second) * second_ref[0]


def slot_kernel(
    grad_ref, left_t_hbm, right_q_hbm, first_rot_hbm, decayed_hbm, left_q_hbm,
    block_hbm, squares_hbm, result_hbm,
    left_t_ref, right_q_ref, first_rot_ref, decayed_ref, left_q_ref,
    block_ref, squares_ref, rotated_ref, result_ref,
    in_sems, block_sems, squares_sems, result_sems,
):
    tile_cols, tile_rows, slots, halves = grad_ref.shape[:4]
    high = tile_rows * SUB
    inputs = (
        (left_t_hbm, left_t_ref),
        (right_q_hbm, right_q_ref),
        (first_rot_hbm, first_rot_ref),
        (decayed_hbm, decayed_ref),
        (left_q_hbm, left_q_ref),
    )
    loads = [
        [
            pltpu.make_async_copy(src.at[k], dst.at[k], in_sems.at[k, i])
            for i, (src, dst) in enumerate(inputs)
        ]
        for k in range(slots)
    ]
    for row in loads:
        for load in row:
            load.start()
    stores = []

    def store(src, dst, sem):
        stores.append(pltpu.make_async_copy(src, dst, sem))
        stores[-1].start()

    def assemble(k):
        return jnp.concatenate(
            [
                jnp.concatenate(
                    [grad_ref[c, :, k, h].reshape(high, LANE) for h in range(halves)], axis=0
                )
                for c in range(tile_cols)
            ],
            axis=1,
        )

    def rotate(k):
        block = assemble(k)
        block_ref[k] = block
        left_grad = jnp.dot(left_t_ref[k], block, preferred_element_type=jnp.float32)
        rotated_ref[k % 2] = jnp.dot(
            left_grad.astype(jnp.bfloat16), right_q_ref[k], preferred_element_type=jnp.float32
        )

    def scale(k):
        rotated = rotated_ref[k % 2]
        share = (2.0 * (1.0 - beta_moment)) * rotated
        squares = decayed_ref[k] + share * rotated
        squares_ref[k] = squares
        root = squares * lax.rsqrt(squares)
        return ((first_rot_ref[k] + share) / (root + 2.0 * epsilon)).astype(jnp.bfloat16)

    def finish(k, scaled):
        turned = lax.dot_general(
            scaled, right_q_ref[k], (((1,), (1,)), ((), ())), preferred_element_type=jnp.float32
        ).astype(jnp.bfloat16)
        result = jnp.dot(left_q_ref[k], turned, preferred_element_type=jnp.float32).astype(
            jnp.bfloat16
        )
        for h in range(halves):
            for c in range(tile_cols):
                result_ref[c, :, k, h] = result[
                    h * high : (h + 1) * high, c * LANE : (c + 1) * LANE
                ].reshape(tile_rows, SUB, LANE)
            store(result_ref.at[:, :, k, h], result_hbm.at[:, :, k, h], result_sems.at[k, h])

    def wait(k, names):
        for i in names:
            loads[k][i].wait()

    wait(0, (0, 1))
    rotate(0)
    for k in range(slots):
        last = k == slots - 1
        store(block_ref.at[k], block_hbm.at[k], block_sems.at[k])
        wait(k, (2, 3, 4))
        if not last:
            wait(k + 1, (0, 1))
            rotate(k + 1)
        scaled = scale(k)
        if last:
            store(squares_ref.at[k], squares_hbm.at[k], squares_sems.at[k])
        finish(k, scaled)
        if not last:
            store(squares_ref.at[k], squares_hbm.at[k], squares_sems.at[k])
    for copy in stores:
        copy.wait()


def per_slot(side):
    return pl.BlockSpec((1, side, side), lambda k: (k, 0, 0))


def near(array):
    return pltpu.with_memory_space_constraint(array, pltpu.VMEM)


def far(array):
    return pltpu.with_memory_space_constraint(array, pltpu.HBM)


def shards(gradient, table, left_stat, right_stat, left_basis, right_basis, moment, second):
    dev_count = lax.axis_size(AXES)
    rows, cols = gradient.shape
    slots, side, _ = left_stat.shape
    halves = side // rows
    tile_cols = side // LANE
    tile_rows = rows // SUB
    blocks = cols // side
    block_cols = lax.axis_size("tp") * blocks
    bf16, f32 = jnp.bfloat16, jnp.float32

    packed = pl.pallas_call(
        pack_kernel,
        out_shape=pltpu.HBM((tile_cols, tile_rows, blocks, SUB, LANE), bf16),
        in_specs=[HBM],
        out_specs=HBM,
        scratch_shapes=[
            pltpu.VMEM((tile_rows, SUB, cols), bf16),
            pltpu.VMEM((tile_cols, tile_rows, blocks, SUB, LANE), bf16),
            pltpu.SemaphoreType.DMA((PARTS,)),
            pltpu.SemaphoreType.DMA((PARTS,)),
        ],
        compiler_params=SMALL,
    )(far(gradient.reshape(tile_rows, SUB, cols)))
    spread = exchange(packed.reshape(dev_count, blocks, SUB, LANE))

    slot_row = state_rows(table, slots)
    block_id = table[:, 0] * block_cols + table[:, 1]
    cell = block_id + table[:, 0] * ((halves - 1) * block_cols)
    targets = jnp.arange(dev_count * slots, dtype=jnp.int32)
    cell_of_row = jnp.sum(
        jnp.where(slot_row[None, :] == targets[:, None], cell[None, :], 0), axis=1
    )
    places = jnp.arange(table.shape[0], dtype=jnp.int32)
    row_of_block = jnp.sum(
        jnp.where(block_id[None, :] == places[:, None], slot_row[None, :], 0), axis=1
    )
    myself = lax.axis_index(AXES)
    count = jnp.sum((table[:, 2] == myself).astype(jnp.int32)).reshape(1)

    state = (slots, side, side)
    left_t, first_rot, decayed = pl.pallas_call(
        prep_kernel,
        grid=(slots,),
        out_shape=[
            jax.ShapeDtypeStruct(state, bf16),
            jax.ShapeDtypeStruct(state, f32),
            jax.ShapeDtypeStruct(state, f32),
        ],
        in_specs=[per_slot(side)] * 4,
        out_specs=[per_slot(side)] * 3,
        cost_estimate=pl.CostEstimate(
            flops=4 * slots * side**3, bytes_accessed=20 * slots * side**2, transcendentals=0
        ),
    )(left_basis, right_basis, moment, second)

    outbox = pl.pallas_call(
        functools.partial(to_owner_kernel, block_cols),
        out_shape=pltpu.HBM((dev_count * slots * halves, SUB, LANE), bf16),
        in_specs=[SMEM, VMEM],
        out_specs=HBM,
        scratch_shapes=[
            pltpu.VMEM((dev_count * slots * halves, SUB, LANE), bf16),
            pltpu.SemaphoreType.DMA((CHUNKS,)),
        ],
        compiler_params=SMALL,
    )(cell_of_row, near(spread.reshape(dev_count * blocks, SUB, LANE)))
    inbox = exchange(outbox.reshape(dev_count, slots, halves, SUB, LANE))

    grad_blocks, squares, results = pl.pallas_call(
        slot_kernel,
        out_shape=[
            jax.ShapeDtypeStruct(state, bf16),
            jax.ShapeDtypeStruct(state, f32),
            pltpu.HBM((tile_cols, tile_rows, slots, halves, SUB, LANE), bf16),
        ],
        in_specs=[VMEM] + [HBM] * 5,
        out_specs=[HBM] * 3,
        scratch_shapes=[
            pltpu.VMEM(state, bf16),
            pltpu.VMEM(state, bf16),
            pltpu.VMEM(state, f32),
            pltpu.VMEM(state, f32),
            pltpu.VMEM(state, bf16),
            pltpu.VMEM(state, bf16),
            pltpu.VMEM(state, f32),
            pltpu.VMEM((2, side, side), f32),
            pltpu.VMEM((tile_cols, tile_rows, slots, halves, SUB, LANE), bf16),
            pltpu.SemaphoreType.DMA((slots, 5)),
            pltpu.SemaphoreType.DMA((slots,)),
            pltpu.SemaphoreType.DMA((slots,)),
            pltpu.SemaphoreType.DMA((slots, halves)),
        ],
        compiler_params=pltpu.CompilerParams(vmem_limit_bytes=48 << 20),
        cost_estimate=pl.CostEstimate(
            flops=8 * slots * side**3, bytes_accessed=20 * slots * side**2, transcendentals=0
        ),
    )(
        near(inbox.reshape(tile_cols, tile_rows, slots, halves, SUB, LANE)),
        far(left_t),
        far(right_basis),
        far(first_rot),
        far(decayed),
        far(left_basis),
    )
    returned = exchange(results.reshape(dev_count, slots, halves, SUB, LANE))

    kept = (jnp.arange(slots, dtype=jnp.int32) < count)[:, None, None]
    new_left = jnp.where(
        kept,
        (
            beta_stats * left_stat.astype(f32)
            + (1.0 - beta_stats)
            * jnp.einsum("sik,sjk->sij", grad_blocks, grad_blocks, preferred_element_type=f32)
        ).astype(bf16),
        left_stat,
    )
    new_right = jnp.where(
        kept,
        (
            beta_stats * right_stat.astype(f32)
            + (1.0 - beta_stats)
            * jnp.einsum("ski,skj->sij", grad_blocks, grad_blocks, preferred_element_type=f32)
        ).astype(bf16),
        right_stat,
    )
    new_second = jnp.where(kept, 0.25 * squares, second)
    new_moment = jnp.where(
        kept,
        (
            beta_moment * moment.astype(f32) + (1.0 - beta_moment) * grad_blocks.astype(f32)
        ).astype(bf16),
        moment,
    )

    gathered = pl.pallas_call(
        functools.partial(to_grid_kernel, block_cols),
        out_shape=pltpu.HBM((dev_count * blocks, SUB, LANE), bf16),
        in_specs=[SMEM, VMEM],
        out_specs=HBM,
        scratch_shapes=[
            pltpu.VMEM((dev_count * blocks, SUB, LANE), bf16),
            pltpu.SemaphoreType.DMA((dev_count * blocks // (halves * block_cols),)),
        ],
        compiler_params=SMALL,
    )(row_of_block, near(returned.reshape(dev_count * slots * halves, SUB, LANE)))
    arrived = exchange(gathered.reshape(dev_count, blocks, SUB, LANE))
    update = pl.pallas_call(
        unpack_kernel,
        out_shape=jax.ShapeDtypeStruct((tile_rows, SUB, cols), bf16),
        in_specs=[VMEM],
        out_specs=HBM,
        scratch_shapes=[pltpu.SemaphoreType.DMA((blocks * tile_cols,))],
        compiler_params=SMALL,
    )(near(arrived.reshape(tile_cols, tile_rows, blocks, SUB, LANE))).reshape(rows, cols)
    return (update, new_left, new_right, new_moment, new_second)


def solution(mesh):
    states = P(AXES, None, None)
    window = P("shard", "tp")
    return jax.shard_map(
        shards,
        mesh=mesh,
        in_specs=(window, P()) + (states,) * 6,
        out_specs=(window,) + (states,) * 4,
        check_vma=False,
    )
```

```python
import functools

import jax
import jax.numpy as jnp
from jax import lax
from jax.experimental import pallas as pl
from jax.experimental.pallas import tpu as pltpu
from jax.sharding import PartitionSpec as P

beta_moment = 0.9
beta_second = 0.95
beta_stats = 0.95
epsilon = 1e-08

AXES = ("shard", "tp")
SUB, LANE = 8, 128
VMEM = pl.BlockSpec(memory_space=pltpu.VMEM)
PARTS = 4
CHUNKS = 8
SMALL = pltpu.CompilerParams(vmem_limit_bytes=8 << 20)
HBM = pl.BlockSpec(memory_space=pltpu.HBM)
SMEM = pl.BlockSpec(memory_space=pltpu.SMEM)


def exchange(array):
    return lax.all_to_all(array, AXES, split_axis=0, concat_axis=0, tiled=True)


def state_rows(table, slots):
    owners = table[:, 2]
    order = jnp.arange(owners.shape[0], dtype=jnp.int32)
    earlier = (owners[None, :] == owners[:, None]) & (order[None, :] < order[:, None])
    return owners * slots + jnp.sum(earlier.astype(jnp.int32), axis=1)


def pack_kernel(grad_ref, out_ref, held_ref, packed_ref, load_sems, store_sems):
    tile_cols, tile_rows, blocks = out_ref.shape[:3]
    parts = load_sems.shape[0]
    step = tile_rows // parts
    loads, stores = [], []
    for r in range(parts):
        at = pl.ds(r * step, step)
        loads.append(pltpu.make_async_copy(grad_ref.at[at], held_ref.at[at], load_sems.at[r]))
        stores.append(
            pltpu.make_async_copy(packed_ref.at[:, at], out_ref.at[:, at], store_sems.at[r])
        )
        loads[-1].start()
    for r in range(parts):
        loads[r].wait()
        rows = slice(r * step, (r + 1) * step)
        for j in range(blocks):
            for c in range(tile_cols):
                at = (j * tile_cols + c) * LANE
                packed_ref[c, rows, j] = held_ref[rows, :, at : at + LANE]
        stores[r].start()
    for store in stores:
        store.wait()


def unpack_kernel(in_ref, out_ref, sems):
    tile_cols, _, blocks = in_ref.shape[:3]
    copies = []
    for j in range(blocks):
        for c in range(tile_cols):
            at = j * tile_cols + c
            copies.append(
                pltpu.make_async_copy(
                    in_ref.at[c, :, j], out_ref.at[:, :, at * LANE : (at + 1) * LANE], sems.at[at]
                )
            )
            copies[-1].start()
    for copy in copies:
        copy.wait()


def to_owner_kernel(half_step, cell_ref, in_ref, out_hbm, out_ref, sems):
    chunks = sems.shape[0]
    rows = cell_ref.shape[0] // chunks
    stores = []
    for r in range(chunks):
        for n in range(r * rows, (r + 1) * rows):
            a = cell_ref[n]
            out_ref[2 * n] = in_ref[a]
            out_ref[2 * n + 1] = in_ref[a + half_step]
        at = pl.ds(2 * r * rows, 2 * rows)
        stores.append(pltpu.make_async_copy(out_ref.at[at], out_hbm.at[at], sems.at[r]))
        stores[-1].start()
    for store in stores:
        store.wait()


def to_grid_kernel(half_step, row_ref, in_ref, out_hbm, out_ref, sems):
    stores = []
    for r in range(row_ref.shape[0] // half_step):
        base = r * 2 * half_step
        for c in range(half_step):
            b = row_ref[r * half_step + c] * 2
            out_ref[base + c] = in_ref[b]
            out_ref[base + c + half_step] = in_ref[b + 1]
        at = pl.ds(base, 2 * half_step)
        stores.append(pltpu.make_async_copy(out_ref.at[at], out_hbm.at[at], sems.at[r]))
        stores[-1].start()
    for store in stores:
        store.wait()


def prep_kernel(
    left_q_ref, right_q_ref, first_ref, second_ref, left_t_ref, first_rot_ref, decayed_ref
):
    left_t = left_q_ref[0].T
    left_t_ref[0] = left_t
    part = jnp.dot(left_t, first_ref[0], preferred_element_type=jnp.float32).astype(jnp.bfloat16)
    first_rot_ref[0] = (2.0 * beta_moment) * jnp.dot(
        part, right_q_ref[0], preferred_element_type=jnp.float32
    )
    decayed_ref[0] = (4.0 * beta_second) * second_ref[0]


def slot_kernel(
    grad_ref, left_t_hbm, right_q_hbm, first_rot_hbm, decayed_hbm, left_q_hbm,
    block_hbm, squares_hbm, result_hbm,
    left_t_ref, right_q_ref, first_rot_ref, decayed_ref, left_q_ref,
    block_ref, squares_ref, rotated_ref, result_ref,
    in_sems, block_sems, squares_sems, result_sems,
):
    tile_cols, tile_rows, slots, halves = grad_ref.shape[:4]
    high = tile_rows * SUB
    inputs = (
        (left_t_hbm, left_t_ref),
        (right_q_hbm, right_q_ref),
        (first_rot_hbm, first_rot_ref),
        (decayed_hbm, decayed_ref),
        (left_q_hbm, left_q_ref),
    )
    loads = [
        [
            pltpu.make_async_copy(src.at[k], dst.at[k], in_sems.at[k, i])
            for i, (src, dst) in enumerate(inputs)
        ]
        for k in range(slots)
    ]
    for row in loads:
        for load in row:
            load.start()
    stores = []

    def store(src, dst, sem):
        stores.append(pltpu.make_async_copy(src, dst, sem))
        stores[-1].start()

    def assemble(k):
        return jnp.concatenate(
            [
                jnp.concatenate(
                    [grad_ref[c, :, k, h].reshape(high, LANE) for h in range(halves)], axis=0
                )
                for c in range(tile_cols)
            ],
            axis=1,
        )

    def rotate(k):
        block = assemble(k)
        block_ref[k] = block
        left_grad = jnp.dot(left_t_ref[k], block, preferred_element_type=jnp.float32)
        if k == 0:
            wait(0, (1,))
        rotated_ref[k % 2] = jnp.dot(
            left_grad.astype(jnp.bfloat16), right_q_ref[k], preferred_element_type=jnp.float32
        )

    def scale(k):
        rotated = rotated_ref[k % 2]
        share = (2.0 * (1.0 - beta_moment)) * rotated
        squares = decayed_ref[k] + share * rotated
        squares_ref[k] = squares
        root = squares * lax.rsqrt(squares)
        return ((first_rot_ref[k] + share) / (root + 2.0 * epsilon)).astype(jnp.bfloat16)

    def finish(k, scaled):
        turned = lax.dot_general(
            scaled, right_q_ref[k], (((1,), (1,)), ((), ())), preferred_element_type=jnp.float32
        ).astype(jnp.bfloat16)
        turns = halves if k == slots - 1 else 1
        for part in range(turns):
            size = halves // turns
            rows = slice(part * size * high, (part + 1) * size * high)
            result = jnp.dot(
                left_q_ref[k, rows], turned, preferred_element_type=jnp.float32
            ).astype(jnp.bfloat16)
            for n in range(size):
                h = part * size + n
                for c in range(tile_cols):
                    result_ref[c, :, k, h] = result[
                        n * high : (n + 1) * high, c * LANE : (c + 1) * LANE
                    ].reshape(tile_rows, SUB, LANE)
                store(result_ref.at[:, :, k, h], result_hbm.at[:, :, k, h], result_sems.at[k, h])

    def wait(k, names):
        for i in names:
            loads[k][i].wait()

    wait(0, (0,))
    rotate(0)
    for k in range(slots):
        last = k == slots - 1
        store(block_ref.at[k], block_hbm.at[k], block_sems.at[k])
        wait(k, (2, 3, 4))
        if not last:
            wait(k + 1, (0, 1))
            rotate(k + 1)
        scaled = scale(k)
        if last:
            store(squares_ref.at[k], squares_hbm.at[k], squares_sems.at[k])
        finish(k, scaled)
        if not last:
            store(squares_ref.at[k], squares_hbm.at[k], squares_sems.at[k])
    for copy in stores:
        copy.wait()


def per_slot(side):
    return pl.BlockSpec((1, side, side), lambda k: (k, 0, 0))


def near(array):
    return pltpu.with_memory_space_constraint(array, pltpu.VMEM)


def far(array):
    return pltpu.with_memory_space_constraint(array, pltpu.HBM)


def shards(gradient, table, left_stat, right_stat, left_basis, right_basis, moment, second):
    dev_count = lax.axis_size(AXES)
    rows, cols = gradient.shape
    slots, side, _ = left_stat.shape
    halves = side // rows
    tile_cols = side // LANE
    tile_rows = rows // SUB
    blocks = cols // side
    block_cols = lax.axis_size("tp") * blocks
    bf16, f32 = jnp.bfloat16, jnp.float32

    packed = pl.pallas_call(
        pack_kernel,
        out_shape=pltpu.HBM((tile_cols, tile_rows, blocks, SUB, LANE), bf16),
        in_specs=[HBM],
        out_specs=HBM,
        scratch_shapes=[
            pltpu.VMEM((tile_rows, SUB, cols), bf16),
            pltpu.VMEM((tile_cols, tile_rows, blocks, SUB, LANE), bf16),
            pltpu.SemaphoreType.DMA((PARTS,)),
            pltpu.SemaphoreType.DMA((PARTS,)),
        ],
        compiler_params=SMALL,
    )(far(gradient.reshape(tile_rows, SUB, cols)))
    spread = exchange(packed.reshape(dev_count, blocks, SUB, LANE))

    slot_row = state_rows(table, slots)
    block_id = table[:, 0] * block_cols + table[:, 1]
    cell = block_id + table[:, 0] * ((halves - 1) * block_cols)
    targets = jnp.arange(dev_count * slots, dtype=jnp.int32)
    cell_of_row = jnp.sum(
        jnp.where(slot_row[None, :] == targets[:, None], cell[None, :], 0), axis=1
    )
    places = jnp.arange(table.shape[0], dtype=jnp.int32)
    row_of_block = jnp.sum(
        jnp.where(block_id[None, :] == places[:, None], slot_row[None, :], 0), axis=1
    )
    myself = lax.axis_index(AXES)
    count = jnp.sum((table[:, 2] == myself).astype(jnp.int32)).reshape(1)

    state = (slots, side, side)
    left_t, first_rot, decayed = pl.pallas_call(
        prep_kernel,
        grid=(slots,),
        out_shape=[
            jax.ShapeDtypeStruct(state, bf16),
            jax.ShapeDtypeStruct(state, f32),
            jax.ShapeDtypeStruct(state, f32),
        ],
        in_specs=[per_slot(side)] * 4,
        out_specs=[per_slot(side)] * 3,
        cost_estimate=pl.CostEstimate(
            flops=4 * slots * side**3, bytes_accessed=20 * slots * side**2, transcendentals=0
        ),
    )(left_basis, right_basis, moment, second)

    outbox = pl.pallas_call(
        functools.partial(to_owner_kernel, block_cols),
        out_shape=pltpu.HBM((dev_count * slots * halves, SUB, LANE), bf16),
        in_specs=[SMEM, VMEM],
        out_specs=HBM,
        scratch_shapes=[
            pltpu.VMEM((dev_count * slots * halves, SUB, LANE), bf16),
            pltpu.SemaphoreType.DMA((CHUNKS,)),
        ],
        compiler_params=SMALL,
    )(cell_of_row, near(spread.reshape(dev_count * blocks, SUB, LANE)))
    inbox = exchange(outbox.reshape(dev_count, slots, halves, SUB, LANE))

    grad_blocks, squares, results = pl.pallas_call(
        slot_kernel,
        out_shape=[
            jax.ShapeDtypeStruct(state, bf16),
            jax.ShapeDtypeStruct(state, f32),
            pltpu.HBM((tile_cols, tile_rows, slots, halves, SUB, LANE), bf16),
        ],
        in_specs=[VMEM] + [HBM] * 5,
        out_specs=[HBM] * 3,
        scratch_shapes=[
            pltpu.VMEM(state, bf16),
            pltpu.VMEM(state, bf16),
            pltpu.VMEM(state, f32),
            pltpu.VMEM(state, f32),
            pltpu.VMEM(state, bf16),
            pltpu.VMEM(state, bf16),
            pltpu.VMEM(state, f32),
            pltpu.VMEM((2, side, side), f32),
            pltpu.VMEM((tile_cols, tile_rows, slots, halves, SUB, LANE), bf16),
            pltpu.SemaphoreType.DMA((slots, 5)),
            pltpu.SemaphoreType.DMA((slots,)),
            pltpu.SemaphoreType.DMA((slots,)),
            pltpu.SemaphoreType.DMA((slots, halves)),
        ],
        compiler_params=pltpu.CompilerParams(vmem_limit_bytes=48 << 20),
        cost_estimate=pl.CostEstimate(
            flops=8 * slots * side**3, bytes_accessed=20 * slots * side**2, transcendentals=0
        ),
    )(
        near(inbox.reshape(tile_cols, tile_rows, slots, halves, SUB, LANE)),
        far(left_t),
        far(right_basis),
        far(first_rot),
        far(decayed),
        far(left_basis),
    )
    returned = exchange(results.reshape(dev_count, slots, halves, SUB, LANE))

    kept = (jnp.arange(slots, dtype=jnp.int32) < count)[:, None, None]
    new_left = jnp.where(
        kept,
        (
            beta_stats * left_stat.astype(f32)
            + (1.0 - beta_stats)
            * jnp.einsum("sik,sjk->sij", grad_blocks, grad_blocks, preferred_element_type=f32)
        ).astype(bf16),
        left_stat,
    )
    new_right = jnp.where(
        kept,
        (
            beta_stats * right_stat.astype(f32)
            + (1.0 - beta_stats)
            * jnp.einsum("ski,skj->sij", grad_blocks, grad_blocks, preferred_element_type=f32)
        ).astype(bf16),
        right_stat,
    )
    new_second = jnp.where(kept, 0.25 * squares, second)
    new_moment = jnp.where(
        kept,
        (
            beta_moment * moment.astype(f32) + (1.0 - beta_moment) * grad_blocks.astype(f32)
        ).astype(bf16),
        moment,
    )

    gathered = pl.pallas_call(
        functools.partial(to_grid_kernel, block_cols),
        out_shape=pltpu.HBM((dev_count * blocks, SUB, LANE), bf16),
        in_specs=[SMEM, VMEM],
        out_specs=HBM,
        scratch_shapes=[
            pltpu.VMEM((dev_count * blocks, SUB, LANE), bf16),
            pltpu.SemaphoreType.DMA((dev_count * blocks // (halves * block_cols),)),
        ],
        compiler_params=SMALL,
    )(row_of_block, near(returned.reshape(dev_count * slots * halves, SUB, LANE)))
    arrived = exchange(gathered.reshape(dev_count, blocks, SUB, LANE))
    update = pl.pallas_call(
        unpack_kernel,
        out_shape=jax.ShapeDtypeStruct((tile_rows, SUB, cols), bf16),
        in_specs=[VMEM],
        out_specs=HBM,
        scratch_shapes=[pltpu.SemaphoreType.DMA((blocks * tile_cols,))],
        compiler_params=SMALL,
    )(near(arrived.reshape(tile_cols, tile_rows, blocks, SUB, LANE))).reshape(rows, cols)
    return (update, new_left, new_right, new_moment, new_second)


def solution(mesh):
    states = P(AXES, None, None)
    window = P("shard", "tp")
    return jax.shard_map(
        shards,
        mesh=mesh,
        in_specs=(window, P()) + (states,) * 6,
        out_specs=(window,) + (states,) * 4,
        check_vma=False,
    )
```
